32 devices in a mesh: shard: 4 (over y, x), rep: 8 (over z, core).
Axes of the slice: x: 2, y: 2, z: 4, core: 2. Of those that a mesh axis runs over, the one named last changes fastest.
Arguments:
- tokens: bfloat16 [4, 1024, 960], P('shard', 'rep'), may hold values from -6 to 6
- segment: int32 [4, 1024], P('shard', 'rep'), may hold values from 0 to 2, as said below
- positions: int32 [4, 1024], P('shard', 'rep'), may hold values from 0 to 1023, as said below
- norm_attn: bfloat16 [960], P('shard'), may hold values from 0.5 to 1.5
- w_query: bfloat16 [960, 960], P('shard'), may hold values from -1 to 1
- w_key: bfloat16 [960, 320], P('shard'), may hold values from -1 to 1
- w_value: bfloat16 [960, 320], P('shard'), may hold values from -0.1875 to 0.1875
- w_out: bfloat16 [960, 960], P('shard'), may hold values from -0.75 to 0.75
- norm_mlp: bfloat16 [960], P('shard'), may hold values from 0.5 to 1.5
- w_gate: bfloat16 [960, 2560], P('shard'), may hold values from -0.1875 to 0.1875
- w_up: bfloat16 [960, 2560], P('shard'), may hold values from -0.1875 to 0.1875
- w_down: bfloat16 [2560, 960], P('shard'), may hold values from -0.125 to 0.125
- cotangent: bfloat16 [4, 1024, 960], P('shard', 'rep'), may hold values from -6 to 6
Outputs:
- output: bfloat16 [4, 1024, 960], P('shard', 'rep')
- grad_tokens: bfloat16 [4, 1024, 960], P('shard', 'rep')
- grad_norm_attn: float32 [960], P('shard')
- grad_query: float32 [960, 960], P('shard')
- grad_key: float32 [960, 320], P('shard')
- grad_value: float32 [960, 320], P('shard')
- grad_out: float32 [960, 960], P('shard')
- grad_norm_mlp: float32 [960], P('shard')
- grad_gate: float32 [960, 2560], P('shard')
- grad_up: float32 [960, 2560], P('shard')
- grad_down: float32 [2560, 960], P('shard')
The draws below stay inside these ranges and needn't reach their ends.
Inputs may be any that keep to these rules, and one draw needn't show every extreme that they name: Along each sequence the segment id starts at 0, never falls and changes at most twice. `positions`: positions count from 0 at a sequence's first token and wherever the segment id changes, and rise by one from token to token otherwise.
All inputs are finite; a program needn't handle non-finite values.
Results may differ from the reference program's by a relative error of at most 0.022.
Values may be sent and summed in bfloat16 or wider, within the bound.
No kernel may reach another device: no remote copies, remote signals or barrier semaphores. Data moves between devices by JAX's collectives and lax.ppermute only.
A program may use at most 192 MiB of HBM per device.

```python
import jax
import jax.numpy as jnp
from jax import lax

D = 960
HQ = 15
HK = 5
HD = 64
FF = 2560
LENGTH = 1024
SEQS = 4


def document_bounds(key):
    cut_points = jax.random.randint(jax.random.fold_in(key, 11), (SEQS, 2), 1, LENGTH)
    whole_row = (jnp.arange(SEQS).astype(jnp.int32) == 0)[:, None]
    cut_points = jnp.where(whole_row, LENGTH, cut_points).astype(jnp.int32)
    lower_cut = jnp.min(cut_points, axis=1)[:, None]
    upper_cut = jnp.max(cut_points, axis=1)[:, None]
    position = jnp.arange(LENGTH).astype(jnp.int32)[None, :]
    return (lower_cut, upper_cut, position)


def draw_segment(key, part):
    lower_cut, upper_cut, position = document_bounds(key)
    return ((position >= lower_cut).astype(jnp.int32) + (position >= upper_cut).astype(jnp.int32)).astype(jnp.int32)


def draw_positions(key, part):
    lower_cut, upper_cut, position = document_bounds(key)
    begin = jnp.where(position >= upper_cut, upper_cut, jnp.where(position >= lower_cut, lower_cut, 0))
    return (position - begin).astype(jnp.int32)


def draw_tokens(key, part):
    shape = (SEQS, LENGTH, D)
    values = jax.random.normal(jax.random.fold_in(key, 31), shape, jnp.float32)
    return jnp.clip(values, -6.0, 6.0).astype(jnp.bfloat16)


def draw_w_query(key, part):
    values = jax.random.normal(jax.random.fold_in(key, 41), (D, HQ * HD), jnp.float32) * D ** (-0.5)
    return jnp.clip(values, -1.0, 1.0).astype(jnp.bfloat16)


def draw_w_key(key, part):
    values = jax.random.normal(jax.random.fold_in(key, 42), (D, HK * HD), jnp.float32) * D ** (-0.5)
    return jnp.clip(values, -1.0, 1.0).astype(jnp.bfloat16)


def steps_of(stream_key, extent, split, least, high):
    def one(axis_at, blocks):
        heights = jax.random.uniform(jax.random.fold_in(jax.random.fold_in(stream_key, 6), axis_at), (blocks,), jnp.float32, least / len(split), high / len(split))
        return jnp.repeat(jnp.exp(heights), extent[axis_at] // blocks).reshape((-1,) + (1,) * (len(extent) - axis_at - 1))

    level = one(*split[0])
    for cut in split[1:]:
        level = level * one(*cut)
    return level


def centred(rng, shape, deviation, most, shards=(), kind=jnp.bfloat16):
    values = deviation * jax.random.normal(rng, shape, jnp.float32)
    if shards:
        values = values * steps_of(rng, shape, shards, -0.22, 0.18)
    return jnp.clip(values, -most, most).astype(kind)


def setup_inputs(seed: int = 0) -> dict:
    splits = jax.random.split(jax.random.key(seed), 14)
    tokens = draw_tokens(jax.random.fold_in(splits[13], 71), 0)
    segment = draw_segment(jax.random.fold_in(splits[13], 71), 0)
    positions = draw_positions(jax.random.fold_in(splits[13], 71), 0)
    norm_attn = jnp.clip(1.0 + 0.1 * jax.random.normal(splits[3], (D,), jnp.float32), 0.5, 1.5).astype(jnp.bfloat16)
    w_query = draw_w_query(jax.random.fold_in(splits[13], 71), 0)
    w_key = draw_w_key(jax.random.fold_in(splits[13], 71), 0)
    w_value = centred(splits[6], (D, HK * HD), D ** -0.5, 0.1875, ((0, 4),))
    w_out = centred(splits[7], (HQ * HD, D), HD ** -0.5, 0.75, ((0, 4),))
    norm_mlp = jnp.clip(1.0 + 0.1 * jax.random.normal(splits[8], (D,), jnp.float32), 0.5, 1.5).astype(jnp.bfloat16)
    w_gate = centred(splits[9], (D, FF), D ** -0.5, 0.1875, ((0, 4),))
    w_up = centred(splits[10], (D, FF), D ** -0.5, 0.1875, ((0, 4),))
    w_down = centred(splits[11], (FF, D), FF ** -0.5, 0.125, ((0, 4),))
    cotangent = centred(splits[12], (SEQS, LENGTH, D), 1.0, 6.0, ((0, 4), (1, 8)))
    return {"tokens": tokens, "segment": segment, "positions": positions, "norm_attn": norm_attn, "w_query": w_query, "w_key": w_key, "w_value": w_value, "w_out": w_out, "norm_mlp": norm_mlp, "w_gate": w_gate, "w_up": w_up, "w_down": w_down, "cotangent": cotangent}


EPSILON = 1e-05
THETA_BASE = 100000.0
NEGATIVE = -1e+30

def product(left, right):
    return jnp.dot(left, right, preferred_element_type=jnp.float32)

def rounded(values):
    return lax.optimization_barrier(values.astype(jnp.bfloat16)).astype(jnp.float32)

def rope_tables(position):
    half_dim = HD // 2
    freqs = THETA_BASE ** (-(jnp.arange(half_dim).astype(jnp.float32) * 2.0 / HD))
    angle = position.astype(jnp.float32)[:, None] * freqs[None, :]
    return (jnp.cos(angle), jnp.sin(angle))

def rotate(values, cosine, sine, direction):
    half_dim = HD // 2
    first_half = values[..., :half_dim]
    second_half = values[..., half_dim:]
    cosine = cosine[:, None, :]
    sine = direction * sine[:, None, :]
    return jnp.concatenate([first_half * cosine - second_half * sine, second_half * cosine + first_half * sine], axis=-1)

def norm_forward(values, gain):
    scale_row = lax.rsqrt(lax.optimization_barrier(jnp.mean(values * values, axis=-1, keepdims=True)) + EPSILON)
    normed = values * scale_row
    return (normed, scale_row, normed * gain)

def norm_backward(grad_norm_out, gain, normed, scale_row):
    grad_gain = lax.optimization_barrier(jnp.sum(grad_norm_out * normed, axis=0))
    grad_normed = grad_norm_out * gain
    grad_input = scale_row * (grad_normed - normed * lax.optimization_barrier(jnp.mean(grad_normed * normed, axis=-1, keepdims=True)))
    return (grad_input, grad_gain)

def block_scores(queries, keys_all, segment_all, start, block, length):
    scale = HD ** (-0.5)
    key_index = jnp.arange(length).astype(jnp.int32)
    query_index = start + jnp.arange(block).astype(jnp.int32)
    query_segment = lax.dynamic_slice_in_dim(segment_all, start, block, 0)
    allowed = (key_index[None, :] <= query_index[:, None]) & (segment_all[None, :] == query_segment[:, None])
    allowed = allowed[:, None, None, :]
    score = jnp.einsum('qhgd,khd->qhgk', queries, keys_all) * scale
    return (jnp.where(allowed, score, NEGATIVE), allowed)

def attention_forward(query_rot, key_rot, value_b, segment_all, length):
    block = min(length, 512)
    keys_f = key_rot.astype(jnp.float32)
    values_f = value_b.astype(jnp.float32)

    def one_block(index):
        start = index * block
        queries = lax.dynamic_slice_in_dim(query_rot, start, block, 0).astype(jnp.float32)
        score, allowed = block_scores(queries, keys_f, segment_all, start, block, length)
        peak = lax.optimization_barrier(jnp.max(score, axis=-1))
        weight = jnp.where(allowed, jnp.exp(score - peak[..., None]), 0.0)
        total = lax.optimization_barrier(jnp.sum(weight, axis=-1))
        result = jnp.einsum('qhgk,khd->qhgd', rounded(weight), values_f) / total[..., None]
        return (result, peak + jnp.log(total))
    results, lses = lax.map(one_block, jnp.arange(length // block).astype(jnp.int32))
    group = HQ // HK
    return (results.reshape(length, HK, group, HD), lses.reshape(length, HK, group))

def attention_backward(query_rot, key_rot, value_b, segment_all, lse_all, attn_f, grad_attn, length):
    block = min(length, 512)
    scale = HD ** (-0.5)
    keys_f = key_rot.astype(jnp.float32)
    values_f = value_b.astype(jnp.float32)

    def step(carry, index):
        grad_keys, grad_values = carry
        start = index * block
        queries = lax.dynamic_slice_in_dim(query_rot, start, block, 0).astype(jnp.float32)
        grad_block = lax.dynamic_slice_in_dim(grad_attn, start, block, 0).astype(jnp.float32)
        lse_block = lax.dynamic_slice_in_dim(lse_all, start, block, 0)
        attn_block = lax.dynamic_slice_in_dim(attn_f, start, block, 0)
        score, allowed = block_scores(queries, keys_f, segment_all, start, block, length)
        prob = jnp.where(allowed, jnp.exp(score - lse_block[..., None]), 0.0)
        grad_values = grad_values + jnp.einsum('qhgk,qhgd->khd', rounded(prob), grad_block)
        grad_prob = jnp.einsum('qhgd,khd->qhgk', grad_block, values_f)
        delta = lax.optimization_barrier(jnp.sum(grad_block * attn_block, axis=-1))
        grad_score = rounded(prob * (grad_prob - delta[..., None]))
        grad_query = jnp.einsum('qhgk,khd->qhgd', grad_score, keys_f) * scale
        grad_keys = grad_keys + jnp.einsum('qhgk,qhgd->khd', grad_score, queries) * scale
        return ((grad_keys, grad_values), grad_query)
    zeros = jnp.zeros((length, HK, HD), jnp.float32)
    (grad_keys, grad_values), grad_queries = lax.scan(step, (zeros, zeros), jnp.arange(length // block).astype(jnp.int32))
    return (grad_queries.reshape(length, HQ, HD), grad_keys, grad_values)

def layer(token_rows, segment_row, position_row, cotangent_rows, params):
    gain_attn, full_query, full_key, full_value, full_out, gain_mlp, full_gate, full_up, full_down = params
    length = token_rows.shape[0]
    group = HQ // HK
    gain_attn = gain_attn.astype(jnp.float32)
    gain_mlp = gain_mlp.astype(jnp.float32)
    inputs = token_rows.astype(jnp.float32)
    cosine, sine = rope_tables(position_row)
    normed1, scale1, scaled1 = norm_forward(inputs, gain_attn)
    hidden1 = scaled1.astype(jnp.bfloat16)
    query = product(hidden1, full_query).reshape(length, HQ, HD)
    key_proj = product(hidden1, full_key).reshape(length, HK, HD)
    value_proj = product(hidden1, full_value)
    query_rot = rotate(query, cosine, sine, 1.0).astype(jnp.bfloat16).reshape(length, HK, group, HD)
    key_rot = rotate(key_proj, cosine, sine, 1.0).astype(jnp.bfloat16)
    value_b = value_proj.astype(jnp.bfloat16).reshape(length, HK, HD)
    attn_f, lse_all = attention_forward(query_rot, key_rot, value_b, segment_row, length)
    attn = attn_f.reshape(length, HQ * HD).astype(jnp.bfloat16)
    middle = inputs + product(attn, full_out)
    normed2, scale2, scaled2 = norm_forward(middle, gain_mlp)
    hidden2 = scaled2.astype(jnp.bfloat16)
    gate = product(hidden2, full_gate)
    upward = product(hidden2, full_up)
    sigma = jax.nn.sigmoid(gate)
    inner = (gate * sigma * upward).astype(jnp.bfloat16)
    result = (middle + product(inner, full_down)).astype(jnp.bfloat16)
    grad_y = cotangent_rows.astype(jnp.float32)
    grad_down = product(inner.T, cotangent_rows)
    grad_inner = product(cotangent_rows, full_down.T)
    grad_gate_act = (grad_inner * upward * sigma * (1.0 + gate * (1.0 - sigma))).astype(jnp.bfloat16)
    grad_up_act = (grad_inner * gate * sigma).astype(jnp.bfloat16)
    grad_gate = product(hidden2.T, grad_gate_act)
    grad_up = product(hidden2.T, grad_up_act)
    grad_hidden2 = product(grad_gate_act, full_gate.T) + product(grad_up_act, full_up.T)
    grad_mid_norm, grad_gain_mlp = norm_backward(grad_hidden2, gain_mlp, normed2, scale2)
    grad_middle = grad_y + grad_mid_norm
    grad_mid_b = grad_middle.astype(jnp.bfloat16)
    grad_out = product(attn.T, grad_mid_b)
    grad_attn = product(grad_mid_b, full_out.T).astype(jnp.bfloat16).reshape(length, HK, group, HD)
    grad_q, grad_k, grad_v = attention_backward(query_rot, key_rot, value_b, segment_row, lse_all, attn_f, grad_attn, length)
    grad_q_b = rotate(grad_q, cosine, sine, -1.0).reshape(length, HQ * HD).astype(jnp.bfloat16)
    grad_k_b = rotate(grad_k, cosine, sine, -1.0).reshape(length, HK * HD).astype(jnp.bfloat16)
    grad_v_b = grad_v.reshape(length, HK * HD).astype(jnp.bfloat16)
    grad_query = product(hidden1.T, grad_q_b)
    grad_key = product(hidden1.T, grad_k_b)
    grad_value = product(hidden1.T, grad_v_b)
    grad_hidden1 = product(grad_q_b, full_query.T) + product(grad_k_b, full_key.T) + product(grad_v_b, full_value.T)
    grad_in_norm, grad_gain_attn = norm_backward(grad_hidden1, gain_attn, normed1, scale1)
    grad_inputs = (grad_middle + grad_in_norm).astype(jnp.bfloat16)
    grads = (grad_gain_attn, grad_query, grad_key, grad_value, grad_out, grad_gain_mlp, grad_gate, grad_up, grad_down)
    return (result, grad_inputs, grads)

def reference(tokens, segment, positions, norm_attn, w_query, w_key, w_value, w_out, norm_mlp, w_gate, w_up, w_down, cotangent):
    params = (norm_attn, w_query, w_key, w_value, w_out, norm_mlp, w_gate, w_up, w_down)

    def step(totals, items):
        token_rows, segment_row, position_row, cotangent_rows = items
        result, grad_inputs, grads = layer(token_rows, segment_row, position_row, cotangent_rows, params)
        totals = tuple((total + grad for total, grad in zip(totals, grads)))
        return (totals, (result, grad_inputs))
    init = tuple((jnp.zeros(weight.shape, jnp.float32) for weight in params))
    totals, (results, grad_inputs) = lax.scan(step, init, (tokens, segment, positions, cotangent))
    return (results, grad_inputs) + totals
```

```python
import functools

import jax
import jax.numpy as jnp
from jax import lax
from jax.experimental import pallas as pl
from jax.experimental.pallas import tpu as pltpu
from jax.sharding import PartitionSpec as P

D = 960
HQ = 15
HK = 5
HD = 64
GROUP = HQ // HK
QKV = (HQ + 2 * HK) * HD

EPSILON = 1e-05
THETA_BASE = 100000.0
NEGATIVE = -1e30
SCALE = HD ** (-0.5)
BF = jnp.bfloat16
F32 = jnp.float32


def product(left, right):
    return jnp.dot(left, right, preferred_element_type=F32)


def rope_tables(position):
    half_dim = HD // 2
    freqs = THETA_BASE ** (-(jnp.arange(half_dim).astype(F32) * 2.0 / HD))
    angle = position[:, None] * freqs[None, :]
    return (jnp.cos(angle), jnp.sin(angle))


def rotate(values, cosine, sine, direction):
    half_dim = HD // 2
    first_half = values[..., :half_dim]
    second_half = values[..., half_dim:]
    sine = direction * sine
    return jnp.concatenate(
        [first_half * cosine - second_half * sine, second_half * cosine + first_half * sine],
        axis=-1,
    )


def norm_forward(values, gain):
    scale_row = lax.rsqrt(jnp.mean(values * values, axis=-1, keepdims=True) + EPSILON)
    normed = values * scale_row
    return (normed, scale_row, normed * gain)


def norm_backward(grad_norm_out, gain, normed, scale_row):
    grad_gain = jnp.sum(grad_norm_out * normed, axis=0)
    grad_normed = grad_norm_out * gain
    grad_input = scale_row * (
        grad_normed - normed * jnp.mean(grad_normed * normed, axis=-1, keepdims=True)
    )
    return (grad_input, grad_gain)


def nt(left, right):
    return lax.dot_general(left, right, (((1,), (1,)), ((), ())), preferred_element_type=F32)


def tn(left, right):
    return lax.dot_general(left, right, (((0,), (0,)), ((), ())), preferred_element_type=F32)


def place_pieces(dest, me, core, own, got, rest, rows, block, lanes):
    dest[me] = own
    n = dest.shape[0]
    for k in range(1, n):
        for first, piece in ((0, got[k - 1]), (1, rest[k - 1])):
            value = piece[0:rows, lanes[0] : lanes[1]]

            @pl.when(core == first)
            def _():
                dest[me ^ k, 0:rows, :] = value

            @pl.when(core != first)
            def _():
                dest[me ^ k, block - rows : block, :] = value


def project(value, weight_ref, lanes):
    n, block, _ = weight_ref.shape
    total = None
    for b in range(n):
        term = product(value[:, b * block : (b + 1) * block], weight_ref[b, :, lanes[0] : lanes[1]])
        total = term if total is None else total + term
    return total


def project_back(value, weight_ref):
    return jnp.concatenate([nt(value, weight_ref[b]) for b in range(weight_ref.shape[0])], axis=1)


def turn(value, cosine, sine):
    u, w = value[:, : HD // 2], value[:, HD // 2 :]
    return jnp.concatenate([u * cosine - w * sine, w * cosine + u * sine], axis=-1).astype(BF)


def key_ranks(places, place, core):
    return [2 * (place - s) + core for s in range(places)] + [
        2 * (place - s) + 1 - core for s in range(places)
    ]


def fill_bias(bias_ref, start_ref, scalars, count, places):
    rank, core, place = scalars[2], scalars[1], scalars[3]
    q_index = rank * count + lax.broadcasted_iota(jnp.int32, (count, count), 0)
    start = start_ref[...]
    for slot, key_rank in enumerate(key_ranks(places, place, core)):
        k_index = key_rank * count + lax.broadcasted_iota(jnp.int32, (count, count), 1)
        allowed = (k_index <= q_index) & (k_index >= start)
        bias_ref[:, slot * count : (slot + 1) * count] = jnp.where(allowed, 0.0, NEGATIVE)


def front_kernel(n, places, block, rows, *refs):
    scalars = refs[0]
    held = refs[1 : 1 + 2 * places]
    i = 1 + 2 * places
    gains_own, w_query, w_key, w_value = refs[i : i + 4]
    got = refs[i + 4 : i + 3 + n]
    rest = refs[i + 3 + n : i + 2 + 2 * n]
    i = i + 2 + 2 * n
    cosine_ref, sine_ref, start_ref = refs[i : i + 3]
    q_out, k_out, v_out, o_out, lse_out, attn_out, hidden_out, weight, gain_out = refs[i + 3 : i + 12]
    slots, gains, bias = refs[i + 12 :]
    me, core = scalars[0], scalars[1]
    count = held[0].shape[0]
    length = 2 * places * count
    own = jnp.concatenate([w_query[...], w_key[...], w_value[...]], axis=1)
    place_pieces(weight, me, core, own, got, rest, rows, block, (0, QKV))
    gains[me, :, 0:block] = gains_own[...].astype(F32)
    for k in range(1, n):
        gains[me ^ k, :, 0:block] = got[k - 1][rows : rows + 16, 0:block].astype(F32)
    gain = jnp.concatenate([gains[b, 0:8, 0:block] for b in range(n)], axis=1)
    gain_out[...] = gain
    gain = gain[0:1]
    for slot in range(2 * places):
        slots[slot] = held[slot][...]
    fill_bias(bias, start_ref, scalars, count, places)

    def hidden_of(slot):
        x = slots[slot].astype(F32)
        scale_row = lax.rsqrt(jnp.mean(x * x, axis=-1, keepdims=True) + EPSILON)
        return (x * scale_row * gain).astype(BF)

    def one_slot(slot, carry):
        hidden = hidden_of(slot)
        base = pl.multiple_of(slot * count, count)
        cosine, sine = cosine_ref[pl.ds(base, count), :], sine_ref[pl.ds(base, count), :]
        both = project(hidden, weight, (HQ * HD, QKV))
        for h in range(HK):
            k_out[h, pl.ds(base, count), :] = turn(both[:, h * HD : (h + 1) * HD], cosine, sine)
            v_out[h, pl.ds(base, count), :] = both[:, (HK + h) * HD : (HK + h + 1) * HD].astype(BF)
        return carry

    lax.fori_loop(0, 2 * places, one_slot, 0)
    hidden = hidden_of(0)
    hidden_out[...] = hidden
    query = project(hidden, weight, (0, HQ * HD))
    cosine, sine = cosine_ref[0:count, :], sine_ref[0:count, :]
    for h in range(HQ):
        part = slice(h % GROUP * count, (h % GROUP + 1) * count)
        q_out[h // GROUP, part, :] = turn(query[:, h * HD : (h + 1) * HD], cosine, sine)

    def one_head(g, carry):
        score = nt(q_out[g], k_out[g]) * SCALE
        score = (score.reshape(GROUP, count, length) + bias[...][None]).reshape(GROUP * count, length)
        peak = jnp.max(score, axis=-1, keepdims=True)
        weight_ = jnp.exp(score - peak)
        total = jnp.sum(weight_, axis=-1, keepdims=True)
        o_out[g] = product(weight_.astype(BF), v_out[g]) / total
        lse_out[g] = peak + jnp.log(total)
        return carry

    lax.fori_loop(0, HK, one_head, 0)
    for h in range(HQ):
        part = slice(h % GROUP * count, (h % GROUP + 1) * count)
        attn_out[:, h * HD : (h + 1) * HD] = o_out[h // GROUP, part, :].astype(BF)


VMEM = pl.BlockSpec(memory_space=pltpu.VMEM)
SMEM = pl.BlockSpec(memory_space=pltpu.SMEM)


def shape(dims, kind):
    return jax.ShapeDtypeStruct(dims, kind)


def call(kernel, args, outs, scratch, flops, name):
    moved = sum(a.size * a.dtype.itemsize for a in list(args) + list(outs))
    return pl.pallas_call(
        kernel,
        in_specs=[SMEM] + [VMEM] * (len(args) - 1),
        out_specs=[VMEM] * len(outs),
        out_shape=list(outs),
        scratch_shapes=scratch,
        cost_estimate=pl.CostEstimate(flops=flops, bytes_accessed=moved, transcendentals=0),
        compiler_params=pltpu.CompilerParams(vmem_limit_bytes=60 * 2**20),
        name=name,
    )(*args)


def out_kernel(n, block, rows, lanes, *refs):
    scalars, attn, tokens, gain, w_out = refs[:5]
    got, rest = refs[5 : 4 + n], refs[4 + n : 3 + 2 * n]
    middle_out, hidden_out, weight = refs[3 + 2 * n :]
    place_pieces(weight, scalars[0], scalars[1], w_out[...], got, rest, rows, block, lanes)
    middle = tokens[...].astype(F32) + project(attn[...], weight, (0, D))
    middle_out[...] = middle
    scale_row = lax.rsqrt(jnp.mean(middle * middle, axis=-1, keepdims=True) + EPSILON)
    hidden_out[...] = (middle * scale_row * gain[1:2]).astype(BF)


def mlp_kernel(n, block, rows, columns, *refs):
    scalars = refs[0]
    hidden, cot = refs[1 : 1 + n], refs[1 + n : 1 + 2 * n]
    own, w_down = refs[1 + 2 * n : 3 + 2 * n]
    i = 3 + 2 * n
    got, rest = refs[i : i + n - 1], refs[i + n - 1 : i + 2 * n - 2]
    i += 2 * n - 2
    dh_own, dh_send, y_own, y_send, inner_out, act_out, wide_hidden, wide_cot, weight = refs[i:]
    place_pieces(
        weight, scalars[0], scalars[1], own[...], got, rest, rows, block, (0, 2 * columns)
    )
    count = hidden[0].shape[0]
    for k in range(n):
        wide_hidden[k * count : (k + 1) * count, :] = hidden[k][...]
        wide_cot[k * count : (k + 1) * count, :] = cot[k][...]
    both = project(wide_hidden[...], weight, (0, 2 * columns))
    gate, upward = both[:, :columns], both[:, columns:]
    grad_inner = nt(wide_cot[...], w_down[...])
    sigma = jax.nn.sigmoid(gate)
    swish = gate * sigma
    act_out[:, :columns] = (grad_inner * upward * sigma * (1.0 + gate * (1.0 - sigma))).astype(BF)
    act_out[:, columns:] = (grad_inner * swish).astype(BF)
    inner_out[...] = (swish * upward).astype(BF)
    for b in range(n):
        term = nt(act_out[...], weight[b])
        lanes = slice(b * block, (b + 1) * block)
        dh_own[:, lanes] = term[:count]
        for k in range(1, n):
            dh_send[k - 1, :, lanes] = term[k * count : (k + 1) * count].astype(BF)
    y = product(inner_out[...], w_down[...])
    y_own[...] = y[:count]
    for k in range(1, n):
        y_send[k - 1] = y[k * count : (k + 1) * count].astype(BF)


def attend_back_kernel(places, scalars, q_ref, k_ref, v_ref, g_ref, o_ref, lse_ref, start_ref, dq_ref, keep_ref, give_ref, bias):
    count = g_ref.shape[1] // GROUP

    @pl.when(pl.program_id(0) == 0)
    def _():
        fill_bias(bias, start_ref, scalars, count, places)

    length = k_ref.shape[1]
    queries, keys, values, grad = q_ref[0], k_ref[0], v_ref[0], g_ref[0]
    delta = jnp.sum(grad.astype(F32) * o_ref[0], axis=-1, keepdims=True)
    score = nt(queries, keys) * SCALE - lse_ref[0]
    score = (score.reshape(GROUP, count, length) + bias[...][None]).reshape(GROUP * count, length)
    prob = jnp.exp(score)
    grad_values = tn(prob.astype(BF), grad)
    grad_prob = nt(grad, values)
    grad_score = (prob * (grad_prob - delta)).astype(BF)
    dq_ref[0] = product(grad_score, keys) * SCALE
    grad_keys = tn(grad_score, queries) * SCALE
    both = jnp.concatenate([grad_keys, grad_values], axis=-1)
    keep_ref[0] = both[: length // 2]
    give_ref[0] = both[length // 2 :].astype(BF)


def attend_back(places, scalars, queries, keys, values, grad, attn, lse, start):
    heads, rows, _ = queries.shape
    length = keys.shape[1]
    head = lambda r, w: pl.BlockSpec((1, r, w), lambda h: (h, 0, 0))
    return pl.pallas_call(
        functools.partial(attend_back_kernel, places),
        grid=(heads,),
        in_specs=[
            SMEM,
            head(rows, HD),
            head(length, HD),
            head(length, HD),
            head(rows, HD),
            head(rows, HD),
            head(rows, 1),
            pl.BlockSpec(start.shape, lambda h: (0, 0)),
        ],
        out_specs=[head(rows, HD), head(length // 2, 2 * HD), head(length // 2, 2 * HD)],
        out_shape=[
            shape((heads, rows, HD), F32),
            shape((heads, length // 2, 2 * HD), F32),
            shape((heads, length // 2, 2 * HD), BF),
        ],
        scratch_shapes=[pltpu.VMEM((rows // GROUP, length), F32)],
        cost_estimate=pl.CostEstimate(
            flops=10 * heads * rows * length * HD,
            bytes_accessed=10 * heads * length * HD * 2,
            transcendentals=heads * rows * length,
        ),
        compiler_params=pltpu.CompilerParams(vmem_limit_bytes=60 * 2**20),
        name="attend_back",
    )(scalars, queries, keys, values, grad, attn, lse, start)


def pick(stacked, index):
    return lax.dynamic_index_in_dim(stacked, index, 0, keepdims=False)


def joined(mine, other, bit, axis):
    both = jnp.stack([mine, other], axis=axis)
    flipped = jnp.stack([other, mine], axis=axis)
    out = jnp.where(bit == 0, both, flipped)
    shape = mine.shape[:axis] + (2 * mine.shape[axis],) + mine.shape[axis + 1 :]
    return out.reshape(shape)


def body(
    tokens,
    segment,
    positions,
    norm_attn,
    w_query,
    w_key,
    w_value,
    w_out,
    norm_mlp,
    w_gate,
    w_up,
    w_down,
    cotangent,
):
    count = tokens.shape[1]
    n = lax.axis_size("shard")
    ranks = lax.axis_size("rep")
    places = ranks // 2
    me = lax.axis_index("shard")
    rank = lax.axis_index("rep")
    core = rank % 2
    place = rank // 2
    block = w_query.shape[0]
    half = block // 2
    columns = w_down.shape[0]
    ff = columns * n

    def across(value, k):
        return lax.ppermute(value, "shard", [(a, a ^ k) for a in range(n)])

    def partner(value):
        return lax.ppermute(value, "rep", [(a, a ^ 1) for a in range(ranks)])

    def place_xor(value, b):
        return lax.ppermute(value, "rep", [(a, a ^ (2 * b)) for a in range(ranks)])

    def place_up(value, s):
        return lax.ppermute(value, "rep", [(a, a + 2 * s) for a in range(ranks - 2 * s)])

    def place_down(value, s):
        return lax.ppermute(value, "rep", [(a + 2 * s, a) for a in range(ranks - 2 * s)])

    rows = -(-half // 16) * 16

    def half_rows(value):
        return jnp.where(core == 0, value[:rows], value[block - rows :])

    scalars = jnp.stack([me, core, rank, place]).astype(jnp.int32)
    gains_own = jnp.pad(jnp.stack([norm_attn, norm_mlp]), ((0, 14), (0, 0)))
    first = jnp.concatenate([half_rows(w_query), half_rows(w_key), half_rows(w_value)], axis=1)
    first = jnp.concatenate([first, jnp.pad(gains_own, ((0, 0), (0, QKV - block)))])
    got_first = [across(first, k) for k in range(1, n)]
    rest_first = [partner(g) for g in got_first]

    own_tokens = tokens[0]
    held = [own_tokens] + [place_up(own_tokens, s) for s in range(1, places)]
    held = held + [partner(h) for h in held]
    length = ranks * count

    def columns_of(owner):
        cut = lambda w, b: w[:, b * columns : (b + 1) * columns]
        pairs = [jnp.concatenate([cut(w_gate, b), cut(w_up, b)], axis=1) for b in range(n)]
        return lax.select_n(owner, *pairs)

    own_pair = columns_of(me)
    out_half = half_rows(w_out)
    got_second = [
        across(jnp.concatenate([half_rows(columns_of(me ^ k)), out_half], axis=1), k)
        for k in range(1, n)
    ]
    rest_second = [partner(g) for g in got_second]
    own_cot = cotangent[0]
    got_cot = [across(own_cot, k) for k in range(1, n)]

    own_position = positions[0].astype(jnp.int32)
    own_index = rank * count + jnp.arange(count, dtype=jnp.int32)
    starts = own_index - own_position
    held_rank = jnp.stack(key_ranks(places, place, core))
    held_index = (held_rank[1:, None] * count + jnp.arange(count)[None, :]).reshape(-1)
    held_position = jnp.concatenate([own_position, jnp.maximum(held_index - starts[0], 0)])
    cosine_all, sine_all = rope_tables(held_position.astype(F32))
    cosine, sine = cosine_all[:count], sine_all[:count]
    start = starts[:, None]

    queries, keys, values, attn_heads, lse, attn, hidden1, full_qkv, gains = call(
        functools.partial(front_kernel, n, places, block, rows),
        [scalars, *held, gains_own, w_query, w_key, w_value, *got_first, *rest_first]
        + [cosine_all, sine_all, start],
        [
            shape((HK, GROUP * count, HD), BF),
            shape((HK, length, HD), BF),
            shape((HK, length, HD), BF),
            shape((HK, GROUP * count, HD), F32),
            shape((HK, GROUP * count, 1), F32),
            shape((count, D), BF),
            shape((count, D), BF),
            shape((n, block, QKV), BF),
            shape((8, D), F32),
        ],
        [
            pltpu.VMEM((2 * places, count, D), BF),
            pltpu.VMEM((n, 16, -(-block // 128) * 128), F32),
            pltpu.VMEM((count, length), F32),
        ],
        2 * length * D * 2 * HK * HD,
        "front",
    )
    gain_attn, gain_mlp = gains[0], gains[1]
    middle, hidden2, full_out = call(
        functools.partial(out_kernel, n, block, rows, (2 * columns, 2 * columns + D)),
        [scalars, attn, own_tokens, gains, w_out, *got_second, *rest_second],
        [shape((count, D), F32), shape((count, D), BF), shape((n, block, D), BF)],
        [],
        2 * count * D * D,
        "out",
    )
    full_out = full_out.reshape(D, D)
    full_qkv = full_qkv.reshape(D, QKV)

    got_hidden2 = [across(hidden2, k) for k in range(1, n)]
    wide = n * count
    dh_own, dh_send, y_own, y_send, inner, acts, wide_hidden2, wide_cot = call(
        functools.partial(mlp_kernel, n, block, rows, columns),
        [scalars, hidden2, *got_hidden2, own_cot, *got_cot, own_pair, w_down]
        + [*got_second, *rest_second],
        [
            shape((count, D), F32),
            shape((n - 1, count, D), BF),
            shape((count, D), F32),
            shape((n - 1, count, D), BF),
            shape((wide, columns), BF),
            shape((wide, 2 * columns), BF),
            shape((wide, D), BF),
            shape((wide, D), BF),
        ],
        [pltpu.VMEM((n, block, 2 * columns), BF)],
        2 * wide * D * columns * 6,
        "mlp",
    )
    grad_gate_act, grad_up_act = acts[:, :columns], acts[:, columns:]
    inputs = own_tokens.astype(F32)
    normed1, scale1, _ = norm_forward(inputs, gain_attn)
    normed2, scale2, _ = norm_forward(middle, gain_mlp)

    def scatter(own, send):
        total = own
        for k in range(1, n):
            total = total + across(send[k - 1], k).astype(F32)
        return total

    grad_hidden2 = scatter(dh_own, dh_send)
    result = (middle + scatter(y_own, y_send)).astype(BF)
    grad_mid_norm, grad_gain_mlp = norm_backward(grad_hidden2, gain_mlp, normed2, scale2)
    grad_middle = own_cot.astype(F32) + grad_mid_norm
    grad_mid_b = grad_middle.astype(BF)
    grad_attn = nt(grad_mid_b, full_out).astype(BF)
    grad_heads = (
        grad_attn.reshape(count, HQ, HD).transpose(1, 0, 2).reshape(HK, GROUP * count, HD)
    )
    grad_queries, kv_keep, kv_give = attend_back(
        places, scalars, queries, keys, values, grad_heads, attn_heads, lse, start
    )
    kv_mine = (kv_keep + partner(kv_give).astype(F32)).reshape(HK, places, count, 2 * HD)
    kv_total = kv_mine[:, 0]
    for s in range(1, places):
        kv_total = kv_total + place_down(kv_mine[:, s].astype(BF), s).astype(F32)
    grad_q = rotate(grad_queries.reshape(HQ, count, HD), cosine, sine, -1.0).astype(BF)
    grad_k = rotate(kv_total[..., :HD], cosine, sine, -1.0).astype(BF)
    grad_v = kv_total[..., HD:].astype(BF)
    grad_qkv = jnp.concatenate([grad_q, grad_k, grad_v]).transpose(1, 0, 2).reshape(count, QKV)
    grad_hidden1 = nt(grad_qkv, full_qkv)
    grad_in_norm, grad_gain_attn = norm_backward(grad_hidden1, gain_attn, normed1, scale1)
    grad_inputs = (grad_middle + grad_in_norm).astype(BF)

    odd = place % 2

    def over_places(value):
        keep = pick(value, odd)
        give = pick(value, 1 - odd).astype(BF)
        total = keep + place_xor(give, 1).astype(F32)
        b = 2
        while b < places:
            mine = total.astype(BF)
            total = mine.astype(F32) + place_xor(mine, b).astype(F32)
            b *= 2
        return total.astype(BF)

    def over_cores(value):
        return pick(value, core) + partner(pick(value, 1 - core).astype(BF)).astype(F32)

    def finish(mine, axis):
        mine = joined(mine, place_xor(mine, 1), odd, axis)
        return joined(mine, partner(mine), core, axis)

    grad_down = over_cores(tn(inner, wide_cot).reshape(2, columns // 2, D))
    grad_down = over_places(grad_down.reshape(2, columns // 4, D))
    grad_down = finish(grad_down, 0).astype(F32)

    grad_pair = jnp.stack([tn(wide_hidden2, grad_gate_act), tn(wide_hidden2, grad_up_act)])
    grad_pair = grad_pair.reshape(2, n, 2, half, columns).transpose(2, 0, 1, 3, 4)
    grad_pair = over_places(over_cores(grad_pair))
    rows = jnp.zeros((half, ff), BF)
    for k in range(n):
        part = pick(grad_pair, me ^ k)
        part = across(part, k) if k else part
        rows = lax.dynamic_update_slice_in_dim(rows, part, (me ^ k) * columns, 1)
    other = place_xor(rows, 1)
    rows = jnp.where(odd == 0, jnp.stack([rows, other]), jnp.stack([other, rows]))
    rows = joined(rows, partner(rows), core, 1).astype(F32)
    grad_gate, grad_up = rows[0], rows[1]

    def reduce_all(local, extra):
        width = local.shape[1]
        padded = -(-(block + 1) // 8) * 8
        while padded % 64:
            padded += 8
        tail = jnp.zeros((n, padded - block - 1, width), F32)
        grads = jnp.concatenate([local.reshape(n, block, width), extra[:, None], tail], axis=1)
        grads = over_cores(grads.reshape(n, 2, padded // 2, width).transpose(1, 0, 2, 3))
        total = pick(grads, me)
        for k in range(1, n):
            total = total + across(pick(grads, me ^ k).astype(BF), k).astype(F32)
        total = over_places(total.reshape(2, padded // 4, width))
        return finish(total, 0).astype(F32)

    extra_out = jnp.zeros((n, D), F32)
    extra_out = lax.dynamic_update_slice(extra_out, grad_gain_mlp.reshape(n, block), (0, 0))
    out_sum = reduce_all(tn(attn, grad_mid_b), extra_out)
    extra_qkv = jnp.zeros((n, QKV), F32)
    extra_qkv = lax.dynamic_update_slice(extra_qkv, grad_gain_attn.reshape(n, block), (0, 0))
    qkv_sum = reduce_all(tn(hidden1, grad_qkv), extra_qkv)

    q_end, k_end = HQ * HD, (HQ + HK) * HD
    return (
        result[None],
        grad_inputs[None],
        qkv_sum[block, :block],
        qkv_sum[:block, :q_end],
        qkv_sum[:block, q_end:k_end],
        qkv_sum[:block, k_end:],
        out_sum[:block],
        out_sum[block, :block],
        grad_gate,
        grad_up,
        grad_down,
    )


def solution(mesh):
    rows = P("shard", None)
    placed = (
        P("shard", "rep", None),
        P("shard", "rep"),
        P("shard", "rep"),
        P("shard"),
        rows,
        rows,
        rows,
        rows,
        P("shard"),
        rows,
        rows,
        rows,
        P("shard", "rep", None),
    )
    outputs = (
        P("shard", "rep", None),
        P("shard", "rep", None),
        P("shard"),
        rows,
        rows,
        rows,
        rows,
        P("shard"),
        rows,
        rows,
        rows,
    )
    return jax.shard_map(
        body, mesh=mesh, in_specs=placed, out_specs=outputs, check_vma=False
    )
```

```python
import functools

import jax
import jax.numpy as jnp
from jax import lax
from jax.experimental import pallas as pl
from jax.experimental.pallas import tpu as pltpu
from jax.sharding import PartitionSpec as P

D = 960
HQ = 15
HK = 5
HD = 64
GROUP = HQ // HK
QKV = (HQ + 2 * HK) * HD

EPSILON = 1e-05
THETA_BASE = 100000.0
NEGATIVE = -1e30
SCALE = HD ** (-0.5)
BF = jnp.bfloat16
F32 = jnp.float32


def product(left, right):
    return jnp.dot(left, right, preferred_element_type=F32)


def rope_tables(position):
    half_dim = HD // 2
    freqs = THETA_BASE ** (-(jnp.arange(half_dim).astype(F32) * 2.0 / HD))
    angle = position[:, None] * freqs[None, :]
    return (jnp.cos(angle), jnp.sin(angle))


def nt(left, right):
    return lax.dot_general(left, right, (((1,), (1,)), ((), ())), preferred_element_type=F32)


def tn(left, right):
    return lax.dot_general(left, right, (((0,), (0,)), ((), ())), preferred_element_type=F32)


def place_pieces(dest, me, core, own, got, rest, rows, block, lanes):
    dest[me] = own
    n = dest.shape[0]
    for k in range(1, n):
        for first, piece in ((0, got[k - 1]), (1, rest[k - 1])):
            value = piece[0:rows, lanes[0] : lanes[1]]

            @pl.when(core == first)
            def _():
                dest[me ^ k, 0:rows, :] = value

            @pl.when(core != first)
            def _():
                dest[me ^ k, block - rows : block, :] = value


def project(value, weight_ref, lanes):
    n, block, _ = weight_ref.shape
    total = None
    for b in range(n):
        term = product(value[:, b * block : (b + 1) * block], weight_ref[b, :, lanes[0] : lanes[1]])
        total = term if total is None else total + term
    return total


def project_back(value, weight_ref):
    return jnp.concatenate([nt(value, weight_ref[b]) for b in range(weight_ref.shape[0])], axis=1)


def turn(value, cosine, sine):
    u, w = value[:, : HD // 2], value[:, HD // 2 :]
    return jnp.concatenate([u * cosine - w * sine, w * cosine + u * sine], axis=-1).astype(BF)


def key_ranks(places, place, core):
    return [2 * (place - s) + core for s in range(places)] + [
        2 * (place - s) + 1 - core for s in range(places)
    ]


def fill_bias(bias_ref, start_ref, scalars, count, places):
    rank, core, place = scalars[2], scalars[1], scalars[3]
    q_index = rank * count + lax.broadcasted_iota(jnp.int32, (count, count), 0)
    start = start_ref[...]
    for slot, key_rank in enumerate(key_ranks(places, place, core)):
        k_index = key_rank * count + lax.broadcasted_iota(jnp.int32, (count, count), 1)
        allowed = (k_index <= q_index) & (k_index >= start)
        bias_ref[:, slot * count : (slot + 1) * count] = jnp.where(allowed, 0.0, NEGATIVE)


def front_kernel(n, places, block, rows, *refs):
    scalars = refs[0]
    held = refs[1 : 1 + 2 * places]
    i = 1 + 2 * places
    gains_own, w_query, w_key, w_value = refs[i : i + 4]
    got = refs[i + 4 : i + 3 + n]
    rest = refs[i + 3 + n : i + 2 + 2 * n]
    i = i + 2 + 2 * n
    cosine_ref, sine_ref, start_ref = refs[i : i + 3]
    q_out, k_out, v_out, o_out, lse_out, attn_out, hidden_out, weight, gain_out = refs[i + 3 : i + 12]
    slots, hiddens, gains, bias = refs[i + 12 :]
    me, core = scalars[0], scalars[1]
    count = held[0].shape[0]
    length = 2 * places * count
    own = jnp.concatenate([w_query[...], w_key[...], w_value[...]], axis=1)
    place_pieces(weight, me, core, own, got, rest, rows, block, (0, QKV))
    gains[me, :, 0:block] = gains_own[...].astype(F32)
    for k in range(1, n):
        gains[me ^ k, :, 0:block] = got[k - 1][rows : rows + 16, 0:block].astype(F32)
    gain = jnp.concatenate([gains[b, 0:8, 0:block] for b in range(n)], axis=1)
    gain_out[...] = gain
    gain = gain[0:1]
    for slot in range(2 * places):
        slots[slot] = held[slot][...]
    fill_bias(bias, start_ref, scalars, count, places)

    def hidden_of(slot):
        x = slots[slot].astype(F32)
        scale_row = lax.rsqrt(jnp.mean(x * x, axis=-1, keepdims=True) + EPSILON)
        return (x * scale_row * gain).astype(BF)

    batch = min(4, 2 * places)

    def some_slots(step, carry):
        for j in range(batch):
            hiddens[j * count : (j + 1) * count, :] = hidden_of(step * batch + j)
        base = pl.multiple_of(step * batch * count, count)
        span = pl.ds(base, batch * count)
        cosine, sine = cosine_ref[span, :], sine_ref[span, :]
        both = project(hiddens[...], weight, (HQ * HD, QKV))
        for h in range(HK):
            k_out[h, span, :] = turn(both[:, h * HD : (h + 1) * HD], cosine, sine)
            v_out[h, span, :] = both[:, (HK + h) * HD : (HK + h + 1) * HD].astype(BF)
        return carry

    lax.fori_loop(0, 2 * places // batch, some_slots, 0)
    hidden = hidden_of(0)
    hidden_out[...] = hidden
    query = project(hidden, weight, (0, HQ * HD))
    cosine, sine = cosine_ref[0:count, :], sine_ref[0:count, :]
    for h in range(HQ):
        part = slice(h % GROUP * count, (h % GROUP + 1) * count)
        q_out[h // GROUP, part, :] = turn(query[:, h * HD : (h + 1) * HD], cosine, sine)

    def one_head(g, carry):
        score = nt(q_out[g], k_out[g]) * SCALE
        score = (score.reshape(GROUP, count, length) + bias[...][None]).reshape(GROUP * count, length)
        peak = jnp.max(score, axis=-1, keepdims=True)
        weight_ = jnp.exp(score - peak)
        total = jnp.sum(weight_, axis=-1, keepdims=True)
        o_out[g] = product(weight_.astype(BF), v_out[g]) / total
        lse_out[g] = peak + jnp.log(total)
        return carry

    lax.fori_loop(0, HK, one_head, 0)
    for h in range(HQ):
        part = slice(h % GROUP * count, (h % GROUP + 1) * count)
        attn_out[:, h * HD : (h + 1) * HD] = o_out[h // GROUP, part, :].astype(BF)


VMEM = pl.BlockSpec(memory_space=pltpu.VMEM)
SMEM = pl.BlockSpec(memory_space=pltpu.SMEM)


def shape(dims, kind):
    return jax.ShapeDtypeStruct(dims, kind)


def call(kernel, args, outs, scratch, flops, name):
    moved = sum(a.size * a.dtype.itemsize for a in list(args) + list(outs))
    return pl.pallas_call(
        kernel,
        in_specs=[SMEM] + [VMEM] * (len(args) - 1),
        out_specs=[VMEM] * len(outs),
        out_shape=list(outs),
        scratch_shapes=scratch,
        cost_estimate=pl.CostEstimate(flops=flops, bytes_accessed=moved, transcendentals=0),
        compiler_params=pltpu.CompilerParams(vmem_limit_bytes=60 * 2**20),
        name=name,
    )(*args)


def out_kernel(n, block, rows, lanes, *refs):
    scalars, attn, tokens, gain, w_out = refs[:5]
    got, rest = refs[5 : 4 + n], refs[4 + n : 3 + 2 * n]
    middle_out, hidden_out, weight = refs[3 + 2 * n :]
    place_pieces(weight, scalars[0], scalars[1], w_out[...], got, rest, rows, block, lanes)
    middle = tokens[...].astype(F32) + project(attn[...], weight, (0, D))
    middle_out[...] = middle
    scale_row = lax.rsqrt(jnp.mean(middle * middle, axis=-1, keepdims=True) + EPSILON)
    hidden_out[...] = (middle * scale_row * gain[1:2]).astype(BF)


def mlp_kernel(n, block, rows, columns, *refs):
    scalars = refs[0]
    hidden, cot = refs[1 : 1 + n], refs[1 + n : 1 + 2 * n]
    own, w_down = refs[1 + 2 * n : 3 + 2 * n]
    i = 3 + 2 * n
    got, rest = refs[i : i + n - 1], refs[i + n - 1 : i + 2 * n - 2]
    i += 2 * n - 2
    dh_own, dh_send, y_own, y_send, inner_out, act_out, wide_hidden, wide_cot, weight = refs[i:]
    place_pieces(
        weight, scalars[0], scalars[1], own[...], got, rest, rows, block, (0, 2 * columns)
    )
    count = hidden[0].shape[0]
    for k in range(n):
        wide_hidden[k * count : (k + 1) * count, :] = hidden[k][...]
        wide_cot[k * count : (k + 1) * count, :] = cot[k][...]
    both = project(wide_hidden[...], weight, (0, 2 * columns))
    gate, upward = both[:, :columns], both[:, columns:]
    grad_inner = nt(wide_cot[...], w_down[...])
    sigma = jax.nn.sigmoid(gate)
    swish = gate * sigma
    act_out[:, :columns] = (grad_inner * upward * sigma * (1.0 + gate * (1.0 - sigma))).astype(BF)
    act_out[:, columns:] = (grad_inner * swish).astype(BF)
    inner_out[...] = (swish * upward).astype(BF)
    for b in range(n):
        term = nt(act_out[...], weight[b])
        lanes = slice(b * block, (b + 1) * block)
        dh_own[:, lanes] = term[:count]
        for k in range(1, n):
            dh_send[k - 1, :, lanes] = term[k * count : (k + 1) * count].astype(BF)
    y = product(inner_out[...], w_down[...])
    y_own[...] = y[:count]
    for k in range(1, n):
        y_send[k - 1] = y[k * count : (k + 1) * count].astype(BF)


def split_halves(value, core, rows):
    low, high = value[:rows], value[rows:]
    return jnp.where(core == 0, low, high), jnp.where(core == 0, high, low).astype(BF)


def mlp_grads_kernel(n, block, columns, scalars, hidden, acts, inner, cot, *outs):
    down_keep, down_give, pair_keep, pair_give = outs
    core = scalars[1]
    keep, give = split_halves(tn(inner[...], cot[...]), core, columns // 2)
    quarter = columns // 4
    for j in range(2):
        down_keep[j] = keep[j * quarter : (j + 1) * quarter]
        down_give[j] = give[j * quarter : (j + 1) * quarter]
    for b in range(n):
        grads = tn(hidden[:, b * block : (b + 1) * block], acts[...])
        keep, give = split_halves(grads, core, block // 2)
        for j in range(2):
            pair_keep[j, b] = keep[:, j * columns : (j + 1) * columns]
            pair_give[j, b] = give[:, j * columns : (j + 1) * columns]


def norm_back(grad, gain, value):
    scale_row = lax.rsqrt(jnp.mean(value * value, axis=-1, keepdims=True) + EPSILON)
    normed = value * scale_row
    grad_gain = jnp.sum(grad * normed, axis=0, keepdims=True)
    grad = grad * gain
    grad = scale_row * (grad - normed * jnp.mean(grad * normed, axis=-1, keepdims=True))
    return grad, grad_gain


def turn_back_kernel(n, places, *refs):
    scalars, dh_own = refs[:2]
    got = refs[2 : 1 + n]
    middle, gains, cot, w_out, q_ref, k_ref, v_ref, o_ref, lse_ref = refs[1 + n : 10 + n]
    start_ref, cosine_ref, sine_ref = refs[10 + n : 13 + n]
    middle_out, middle_b_out, gain_out, gq_out, keep_out, give_out = refs[13 + n : 19 + n]
    heads, bias = refs[19 + n :]
    count = dh_own.shape[0]
    grad = dh_own[...]
    for piece in got:
        grad = grad + piece[...].astype(F32)
    grad, grad_gain = norm_back(grad, gains[1:2, :], middle[...])
    gain_out[...] = jnp.broadcast_to(grad_gain, gain_out.shape)
    grad = grad + cot[...].astype(F32)
    middle_out[...] = grad
    grad_b = grad.astype(BF)
    middle_b_out[...] = grad_b
    grad_attn = project_back(grad_b, w_out).astype(BF)
    for h in range(HQ):
        part = slice(h % GROUP * count, (h % GROUP + 1) * count)
        heads[h // GROUP, part, :] = grad_attn[:, h * HD : (h + 1) * HD]
    fill_bias(bias, start_ref, scalars, count, places)
    length = 2 * places * count
    cosine, sine = cosine_ref[...], sine_ref[...]

    for g in range(HK):
        queries, keys, values, grad = q_ref[g], k_ref[g], v_ref[g], heads[g]
        delta = jnp.sum(grad.astype(F32) * o_ref[g], axis=-1, keepdims=True)
        score = nt(queries, keys) * SCALE - lse_ref[g]
        score = score.reshape(GROUP, count, length) + bias[...][None]
        prob = jnp.exp(score.reshape(GROUP * count, length))
        grad_values = tn(prob.astype(BF), grad)
        grad_prob = nt(grad, values)
        grad_score = (prob * (grad_prob - delta)).astype(BF)
        dq = product(grad_score, keys) * SCALE
        for j in range(GROUP):
            h = g * GROUP + j
            gq_out[:, h * HD : (h + 1) * HD] = turn(dq[j * count : (j + 1) * count], cosine, -sine)
        grad_keys = tn(grad_score, queries) * SCALE
        both = jnp.concatenate([grad_keys, grad_values], axis=-1)
        for s in range(places):
            keep_out[s, g] = both[s * count : (s + 1) * count]
            give_out[s, g] = both[(places + s) * count : (places + s + 1) * count].astype(BF)


def padded_rows(block):
    return -(-(block + 1) // 32) * 32


def split_block(grads, gain_row, block, core, keep_ref, give_ref, b):
    rows = padded_rows(block)
    width = grads.shape[1]
    tail = jnp.concatenate(
        [gain_row[:, b * block : (b + 1) * block], jnp.zeros((1, width - block), F32)], axis=1
    )
    tail = jnp.concatenate([tail, jnp.zeros((rows - block - 1, width), F32)])
    keep, give = split_halves(jnp.concatenate([grads, tail]), core, rows // 2)
    keep_ref[b] = keep
    give_ref[b] = give


def out_grads_kernel(n, block, scalars, attn, grad_b, gain_row, keep_out, give_out):
    for b in range(n):
        grads = tn(attn[:, b * block : (b + 1) * block], grad_b[...])
        split_block(grads, gain_row[0:1, :], block, scalars[1], keep_out, give_out, b)


def final_kernel(n, block, *refs):
    scalars, kv_own, gq, cosine_ref, sine_ref, weight, hidden, tokens, gains, middle = refs[:10]
    got = refs[10:-4]
    tokens_out, keep_out, give_out, grad_ref = refs[-4:]
    grad_ref[:, : HQ * HD] = gq[...]
    cosine, sine = cosine_ref[...], sine_ref[...]
    for h in range(HK):
        total = kv_own[h]
        for piece in got:
            total = total + piece[h].astype(F32)
        base = HQ * HD + h * HD
        grad_ref[:, base : base + HD] = turn(total[:, :HD], cosine, -sine)
        base += HK * HD
        grad_ref[:, base : base + HD] = total[:, HD:].astype(BF)
    grad_qkv = grad_ref[...]
    grad = project_back(grad_qkv, weight)
    grad, grad_gain = norm_back(grad, gains[0:1, :], tokens[...].astype(F32))
    tokens_out[...] = (middle[...] + grad).astype(BF)
    for b in range(n):
        grads = tn(hidden[:, b * block : (b + 1) * block], grad_qkv)
        split_block(grads, grad_gain, block, scalars[1], keep_out, give_out, b)


def fold_kernel(order, keep, recv, own, *gives):
    own[...] = keep[order[0]] + recv[order[0]].astype(F32)
    for j, give in enumerate(gives):
        give[...] = (keep[order[j + 1]] + recv[order[j + 1]].astype(F32)).astype(BF)


def fold(keep, recv, order):
    rest = keep.shape[1:]
    outs = [shape(rest, F32)] + [shape(rest, BF)] * (keep.shape[0] - 1)
    order = jnp.stack([jnp.int32(o) for o in order])
    return call(fold_kernel, [order, keep, recv], outs, [], keep.size, "fold")


def pick(stacked, index):
    return lax.dynamic_index_in_dim(stacked, index, 0, keepdims=False)


def joined(mine, other, bit, axis):
    both = jnp.stack([mine, other], axis=axis)
    flipped = jnp.stack([other, mine], axis=axis)
    out = jnp.where(bit == 0, both, flipped)
    shape = mine.shape[:axis] + (2 * mine.shape[axis],) + mine.shape[axis + 1 :]
    return out.reshape(shape)


def body(
    tokens,
    segment,
    positions,
    norm_attn,
    w_query,
    w_key,
    w_value,
    w_out,
    norm_mlp,
    w_gate,
    w_up,
    w_down,
    cotangent,
):
    count = tokens.shape[1]
    n = lax.axis_size("shard")
    ranks = lax.axis_size("rep")
    places = ranks // 2
    me = lax.axis_index("shard")
    rank = lax.axis_index("rep")
    core = rank % 2
    place = rank // 2
    block = w_query.shape[0]
    half = block // 2
    columns = w_down.shape[0]
    ff = columns * n

    def across(value, k):
        return lax.ppermute(value, "shard", [(a, a ^ k) for a in range(n)])

    def partner(value):
        return lax.ppermute(value, "rep", [(a, a ^ 1) for a in range(ranks)])

    def place_xor(value, b):
        return lax.ppermute(value, "rep", [(a, a ^ (2 * b)) for a in range(ranks)])

    def place_up(value, s):
        return lax.ppermute(value, "rep", [(a, a + 2 * s) for a in range(ranks - 2 * s)])

    def place_down(value, s):
        return lax.ppermute(value, "rep", [(a + 2 * s, a) for a in range(ranks - 2 * s)])

    rows = -(-half // 16) * 16

    def half_rows(value):
        return jnp.where(core == 0, value[:rows], value[block - rows :])

    scalars = jnp.stack([me, core, rank, place]).astype(jnp.int32)
    gains_own = jnp.pad(jnp.stack([norm_attn, norm_mlp]), ((0, 14), (0, 0)))
    first = jnp.concatenate([half_rows(w_query), half_rows(w_key), half_rows(w_value)], axis=1)
    first = jnp.concatenate([first, jnp.pad(gains_own, ((0, 0), (0, QKV - block)))])
    got_first = [across(first, k) for k in range(1, n)]
    rest_first = [partner(g) for g in got_first]

    own_tokens = tokens[0]
    held = [own_tokens] + [place_up(own_tokens, s) for s in range(1, places)]
    held = held + [partner(h) for h in held]
    length = ranks * count

    def columns_of(owner):
        cut = lambda w, b: w[:, b * columns : (b + 1) * columns]
        pairs = [jnp.concatenate([cut(w_gate, b), cut(w_up, b)], axis=1) for b in range(n)]
        return lax.select_n(owner, *pairs)

    own_pair = columns_of(me)
    out_half, _ = lax.optimization_barrier((half_rows(w_out), got_first))
    got_second = [
        across(jnp.concatenate([half_rows(columns_of(me ^ k)), out_half], axis=1), k)
        for k in range(1, n)
    ]

    own_position = positions[0].astype(jnp.int32)
    own_index = rank * count + jnp.arange(count, dtype=jnp.int32)
    starts = own_index - own_position
    held_rank = jnp.stack(key_ranks(places, place, core))
    held_index = (held_rank[1:, None] * count + jnp.arange(count)[None, :]).reshape(-1)
    held_position = jnp.concatenate([own_position, jnp.maximum(held_index - starts[0], 0)])
    cosine_all, sine_all = rope_tables(held_position.astype(F32))
    cosine, sine = cosine_all[:count], sine_all[:count]
    start = starts[:, None]

    queries, keys, values, attn_heads, lse, attn, hidden1, full_qkv, gains = call(
        functools.partial(front_kernel, n, places, block, rows),
        [scalars, *held, gains_own, w_query, w_key, w_value, *got_first, *rest_first]
        + [cosine_all, sine_all, start],
        [
            shape((HK, GROUP * count, HD), BF),
            shape((HK, length, HD), BF),
            shape((HK, length, HD), BF),
            shape((HK, GROUP * count, HD), F32),
            shape((HK, GROUP * count, 1), F32),
            shape((count, D), BF),
            shape((count, D), BF),
            shape((n, block, QKV), BF),
            shape((8, D), F32),
        ],
        [
            pltpu.VMEM((2 * places, count, D), BF),
            pltpu.VMEM((min(4, 2 * places) * count, D), BF),
            pltpu.VMEM((n, 16, -(-block // 128) * 128), F32),
            pltpu.VMEM((count, length), F32),
        ],
        2 * length * D * 2 * HK * HD,
        "front",
    )
    attn, got_second, own_cot = lax.optimization_barrier((attn, got_second, cotangent[0]))
    rest_second = [partner(g) for g in got_second]
    got_cot = [across(own_cot, k) for k in range(1, n)]
    middle, hidden2, full_out = call(
        functools.partial(out_kernel, n, block, rows, (2 * columns, 2 * columns + D)),
        [scalars, attn, own_tokens, gains, w_out, *got_second, *rest_second],
        [shape((count, D), F32), shape((count, D), BF), shape((n, block, D), BF)],
        [],
        2 * count * D * D,
        "out",
    )

    got_hidden2 = [across(hidden2, k) for k in range(1, n)]
    wide = n * count
    dh_own, dh_send, y_own, y_send, inner, acts, wide_hidden2, wide_cot = call(
        functools.partial(mlp_kernel, n, block, rows, columns),
        [scalars, hidden2, *got_hidden2, own_cot, *got_cot, own_pair, w_down]
        + [*got_second, *rest_second],
        [
            shape((count, D), F32),
            shape((n - 1, count, D), BF),
            shape((count, D), F32),
            shape((n - 1, count, D), BF),
            shape((wide, columns), BF),
            shape((wide, 2 * columns), BF),
            shape((wide, D), BF),
            shape((wide, D), BF),
        ],
        [pltpu.VMEM((n, block, 2 * columns), BF)],
        2 * wide * D * columns * 6,
        "mlp",
    )
    got_dh = [across(dh_send[k - 1], k) for k in range(1, n)]
    down_keep, down_give, pair_keep, pair_give = call(
        functools.partial(mlp_grads_kernel, n, block, columns),
        [scalars, wide_hidden2, acts, inner, wide_cot],
        [
            shape((2, columns // 4, D), F32),
            shape((2, columns // 4, D), BF),
            shape((2, n, half, columns), F32),
            shape((2, n, half, columns), BF),
        ],
        [],
        2 * wide * D * columns * 3,
        "mlp_grads",
    )
    grad_middle, grad_mid_b, gain_mlp_row, gq, kv_keep, kv_give = call(
        functools.partial(turn_back_kernel, n, places),
        [scalars, dh_own, *got_dh, middle, gains, own_cot, full_out, queries, keys, values]
        + [attn_heads, lse, start, cosine, sine],
        [
            shape((count, D), F32),
            shape((count, D), BF),
            shape((8, D), F32),
            shape((count, D), BF),
            shape((places, HK, count, 2 * HD), F32),
            shape((places, HK, count, 2 * HD), BF),
        ],
        [pltpu.VMEM((HK, GROUP * count, HD), BF), pltpu.VMEM((count, length), F32)],
        10 * HQ * count * length * HD,
        "turn_back",
    )
    kv_sums = fold(kv_keep, partner(kv_give), list(range(places)))
    got_kv = [place_down(kv_sums[s], s) for s in range(1, places)]
    y_total = y_own
    for k in range(1, n):
        y_total = y_total + across(y_send[k - 1], k).astype(F32)
    result = (middle + y_total).astype(BF)
    padded = padded_rows(block)
    out_keep, out_give = call(
        functools.partial(out_grads_kernel, n, block),
        [scalars, attn, grad_mid_b, gain_mlp_row],
        [shape((n, padded // 2, D), F32), shape((n, padded // 2, D), BF)],
        [],
        2 * count * D * D,
        "out_grads",
    )
    grad_inputs, qkv_keep, qkv_give = call(
        functools.partial(final_kernel, n, block),
        [scalars, kv_sums[0], gq, cosine, sine, full_qkv, hidden1, own_tokens, gains, grad_middle]
        + got_kv,
        [
            shape((count, D), BF),
            shape((n, padded // 2, QKV), F32),
            shape((n, padded // 2, QKV), BF),
        ],
        [pltpu.VMEM((count, QKV), BF)],
        4 * count * D * QKV,
        "final",
    )

    odd = place % 2

    def over_places(keep, recv):
        keep, give = fold(keep, recv, [odd, 1 - odd])
        total = keep + place_xor(give, 1).astype(F32)
        b = 2
        while b < places:
            mine = total.astype(BF)
            total = mine.astype(F32) + place_xor(mine, b).astype(F32)
            b *= 2
        return total.astype(BF)

    def finish(mine, axis):
        mine = joined(mine, place_xor(mine, 1), odd, axis)
        return joined(mine, partner(mine), core, axis)

    grad_down = finish(over_places(down_keep, partner(down_give)), 0).astype(F32)

    grad_pair = over_places(pair_keep, partner(pair_give))
    pair_rows = jnp.zeros((half, ff), BF)
    for k in range(n):
        part = pick(grad_pair, me ^ k)
        part = across(part, k) if k else part
        pair_rows = lax.dynamic_update_slice_in_dim(pair_rows, part, (me ^ k) * columns, 1)
    other = place_xor(pair_rows, 1)
    pair_rows = jnp.where(
        odd == 0, jnp.stack([pair_rows, other]), jnp.stack([other, pair_rows])
    )
    pair_rows = joined(pair_rows, partner(pair_rows), core, 1).astype(F32)
    grad_gate, grad_up = pair_rows[0], pair_rows[1]

    def reduce_all(keep, give):
        total, *gives = fold(keep, partner(give), [me ^ k for k in range(n)])
        recv = [across(g, k) for k, g in enumerate(gives, 1)]
        quarter = padded // 4
        total = total + sum(r.astype(F32) for r in recv[:-1])
        width = total.shape[1]
        total = over_places(total.reshape(2, quarter, width), recv[-1].reshape(2, quarter, width))
        return finish(total, 0).astype(F32)

    out_sum = reduce_all(out_keep, out_give)
    qkv_sum = reduce_all(qkv_keep, qkv_give)

    q_end, k_end = HQ * HD, (HQ + HK) * HD
    return (
        result[None],
        grad_inputs[None],
        qkv_sum[block, :block],
        qkv_sum[:block, :q_end],
        qkv_sum[:block, q_end:k_end],
        qkv_sum[:block, k_end:],
        out_sum[:block],
        out_sum[block, :block],
        grad_gate,
        grad_up,
        grad_down,
    )


def solution(mesh):
    rows = P("shard", None)
    placed = (
        P("shard", "rep", None),
        P("shard", "rep"),
        P("shard", "rep"),
        P("shard"),
        rows,
        rows,
        rows,
        rows,
        P("shard"),
        rows,
        rows,
        rows,
        P("shard", "rep", None),
    )
    outputs = (
        P("shard", "rep", None),
        P("shard", "rep", None),
        P("shard"),
        rows,
        rows,
        rows,
        rows,
        P("shard"),
        rows,
        rows,
        rows,
    )
    return jax.shard_map(
        body, mesh=mesh, in_specs=placed, out_specs=outputs, check_vma=False
    )
```

```python
import functools

import jax
import jax.numpy as jnp
from jax import lax
from jax.experimental import pallas as pl
from jax.experimental.layout import Layout, with_layout_constraint
from jax.experimental.pallas import tpu as pltpu
from jax.sharding import PartitionSpec as P

D = 960
HQ = 15
HK = 5
HD = 64
GROUP = HQ // HK
QKV = (HQ + 2 * HK) * HD

EPSILON = 1e-05
THETA_BASE = 100000.0
NEGATIVE = -1e30
SCALE = HD ** (-0.5)
BF = jnp.bfloat16
F32 = jnp.float32


def product(left, right):
    return jnp.dot(left, right, preferred_element_type=F32)


def rope_tables(position):
    half_dim = HD // 2
    freqs = THETA_BASE ** (-(jnp.arange(half_dim).astype(F32) * 2.0 / HD))
    angle = position[:, None] * freqs[None, :]
    return (jnp.cos(angle), jnp.sin(angle))


def nt(left, right):
    return lax.dot_general(left, right, (((1,), (1,)), ((), ())), preferred_element_type=F32)


def tn(left, right):
    return lax.dot_general(left, right, (((0,), (0,)), ((), ())), preferred_element_type=F32)


def place_pieces(dest, me, core, own, got, rest, rows, block, lanes):
    dest[me] = own
    n = dest.shape[0]
    for k in range(1, n):
        for first, piece in ((0, got[k - 1]), (1, rest[k - 1])):
            value = piece[0:rows, lanes[0] : lanes[1]]

            @pl.when(core == first)
            def _():
                dest[me ^ k, 0:rows, :] = value

            @pl.when(core != first)
            def _():
                dest[me ^ k, block - rows : block, :] = value


def project(value, weight_ref, lanes):
    n, block, _ = weight_ref.shape
    total = None
    for b in range(n):
        term = product(value[:, b * block : (b + 1) * block], weight_ref[b, :, lanes[0] : lanes[1]])
        total = term if total is None else total + term
    return total


def project_back(value, weight_ref):
    return jnp.concatenate([nt(value, weight_ref[b]) for b in range(weight_ref.shape[0])], axis=1)


def turn(value, cosine, sine):
    u, w = value[:, : HD // 2], value[:, HD // 2 :]
    return jnp.concatenate([u * cosine - w * sine, w * cosine + u * sine], axis=-1).astype(BF)


def key_ranks(places, place, core):
    return [2 * (place - s) + core for s in range(places)] + [
        2 * (place - s) + 1 - core for s in range(places)
    ]


def fill_bias(bias_ref, start_ref, scalars, count, places):
    rank, core, place = scalars[2], scalars[1], scalars[3]
    q_index = rank * count + lax.broadcasted_iota(jnp.int32, (count, count), 0)
    start = start_ref[...]
    for slot, key_rank in enumerate(key_ranks(places, place, core)):
        k_index = key_rank * count + lax.broadcasted_iota(jnp.int32, (count, count), 1)
        allowed = (k_index <= q_index) & (k_index >= start)
        bias_ref[:, slot * count : (slot + 1) * count] = jnp.where(allowed, 0.0, NEGATIVE)


def front_kernel(n, places, block, rows, *refs):
    scalars = refs[0]
    held = refs[1 : 1 + 2 * places]
    i = 1 + 2 * places
    gains_own, w_query, w_key, w_value = refs[i : i + 4]
    got = refs[i + 4 : i + 3 + n]
    rest = refs[i + 3 + n : i + 2 + 2 * n]
    i = i + 2 + 2 * n
    cosine_ref, sine_ref, start_ref = refs[i : i + 3]
    q_out, k_out, v_out, o_out, lse_out, attn_out, hidden_out, weight, gain_out = refs[i + 3 : i + 12]
    slots, hiddens, gains, bias = refs[i + 12 :]
    me, core = scalars[0], scalars[1]
    count = held[0].shape[0]
    length = 2 * places * count
    own = jnp.concatenate([w_query[...], w_key[...], w_value[...]], axis=1)
    place_pieces(weight, me, core, own, got, rest, rows, block, (0, QKV))
    gains[me, :, 0:block] = gains_own[...].astype(F32)
    for k in range(1, n):
        gains[me ^ k, :, 0:block] = got[k - 1][rows : rows + 16, 0:block].astype(F32)
    gain = jnp.concatenate([gains[b, 0:8, 0:block] for b in range(n)], axis=1)
    gain_out[...] = gain
    gain = gain[0:1]
    for slot in range(2 * places):
        slots[slot] = held[slot][...]
    fill_bias(bias, start_ref, scalars, count, places)

    def hidden_of(slot):
        x = slots[slot].astype(F32)
        scale_row = lax.rsqrt(jnp.mean(x * x, axis=-1, keepdims=True) + EPSILON)
        return (x * scale_row * gain).astype(BF)

    batch = min(4, 2 * places)

    def some_slots(step, carry):
        for j in range(batch):
            hiddens[j * count : (j + 1) * count, :] = hidden_of(step * batch + j)
        base = pl.multiple_of(step * batch * count, count)
        span = pl.ds(base, batch * count)
        cosine, sine = cosine_ref[span, :], sine_ref[span, :]
        both = project(hiddens[...], weight, (HQ * HD, QKV))
        for h in range(HK):
            k_out[h, span, :] = turn(both[:, h * HD : (h + 1) * HD], cosine, sine)
            v_out[h, span, :] = both[:, (HK + h) * HD : (HK + h + 1) * HD].astype(BF)
        return carry

    lax.fori_loop(0, 2 * places // batch, some_slots, 0)
    hidden = hidden_of(0)
    hidden_out[...] = hidden
    query = project(hidden, weight, (0, HQ * HD))
    cosine, sine = cosine_ref[0:count, :], sine_ref[0:count, :]
    for h in range(HQ):
        part = slice(h % GROUP * count, (h % GROUP + 1) * count)
        turned = turn(query[:, h * HD : (h + 1) * HD], cosine, sine)
        q_out[h // GROUP, part, :] = turned * BF(SCALE)

    def one_head(g, carry):
        score = nt(q_out[g], k_out[g])
        score = (score.reshape(GROUP, count, length) + bias[...][None]).reshape(GROUP * count, length)
        peak = jnp.max(score, axis=-1, keepdims=True)
        weight_ = jnp.exp(score - peak)
        total = jnp.sum(weight_, axis=-1, keepdims=True)
        o_out[g] = product(weight_.astype(BF), v_out[g]) / total
        lse_out[g] = peak + jnp.log(total)
        return carry

    lax.fori_loop(0, HK, one_head, 0)
    for h in range(HQ):
        part = slice(h % GROUP * count, (h % GROUP + 1) * count)
        attn_out[:, h * HD : (h + 1) * HD] = o_out[h // GROUP, part, :].astype(BF)


VMEM = pl.BlockSpec(memory_space=pltpu.VMEM)
SMEM = pl.BlockSpec(memory_space=pltpu.SMEM)


def shape(dims, kind):
    return jax.ShapeDtypeStruct(dims, kind)


def call(kernel, args, outs, scratch, flops):
    moved = sum(a.size * a.dtype.itemsize for a in list(args) + list(outs))
    return pl.pallas_call(
        kernel,
        in_specs=[SMEM] + [VMEM] * (len(args) - 1),
        out_specs=[VMEM] * len(outs),
        out_shape=list(outs),
        scratch_shapes=scratch,
        cost_estimate=pl.CostEstimate(flops=flops, bytes_accessed=moved, transcendentals=0),
        compiler_params=pltpu.CompilerParams(vmem_limit_bytes=60 * 2**20),
    )(*args)


def out_kernel(n, block, rows, lanes, *refs):
    scalars, attn, tokens, gain, w_out = refs[:5]
    got, rest = refs[5 : 4 + n], refs[4 + n : 3 + 2 * n]
    middle_out, hidden_out, weight = refs[3 + 2 * n :]
    place_pieces(weight, scalars[0], scalars[1], w_out[...], got, rest, rows, block, lanes)
    middle = tokens[...].astype(F32) + project(attn[...], weight, (0, D))
    middle_out[...] = middle
    scale_row = lax.rsqrt(jnp.mean(middle * middle, axis=-1, keepdims=True) + EPSILON)
    hidden_out[...] = (middle * scale_row * gain[1:2]).astype(BF)


def mlp_kernel(n, block, rows, columns, *refs):
    scalars = refs[0]
    hidden, cot = refs[1 : 1 + n], refs[1 + n : 1 + 2 * n]
    own, w_down = refs[1 + 2 * n : 3 + 2 * n]
    i = 3 + 2 * n
    got, rest = refs[i : i + n - 1], refs[i + n - 1 : i + 2 * n - 2]
    i += 2 * n - 2
    dh_own, dh_send = refs[i], refs[i + 1 : i + n]
    inner_out, act_out, wide_hidden, wide_cot, weight = refs[i + n :]
    place_pieces(
        weight, scalars[0], scalars[1], own[...], got, rest, rows, block, (0, 2 * columns)
    )
    count = hidden[0].shape[0]
    for k in range(n):
        wide_hidden[k * count : (k + 1) * count, :] = hidden[k][...]
        wide_cot[k * count : (k + 1) * count, :] = cot[k][...]
    both = project(wide_hidden[...], weight, (0, 2 * columns))
    gate, upward = both[:, :columns], both[:, columns:]
    grad_inner = nt(wide_cot[...], w_down[...])
    sigma = jax.nn.sigmoid(gate)
    swish = gate * sigma
    act_out[:, :columns] = (grad_inner * upward * sigma * (1.0 + gate * (1.0 - sigma))).astype(BF)
    act_out[:, columns:] = (grad_inner * swish).astype(BF)
    inner_out[...] = (swish * upward).astype(BF)
    for b in range(n):
        term = nt(act_out[...], weight[b])
        lanes = slice(b * block, (b + 1) * block)
        dh_own[:, lanes] = term[:count]
        for k in range(1, n):
            dh_send[k - 1][:, lanes] = term[k * count : (k + 1) * count].astype(BF)


def split_halves(value, core, rows):
    low, high = value[:rows], value[rows:]
    return jnp.where(core == 0, low, high), jnp.where(core == 0, high, low).astype(BF)


def mlp_grads_kernel(n, block, columns, scalars, hidden, acts, inner, cot, w_down, *outs):
    down_keep, down_give, pair_keep, pair_give, y_own = outs[:5]
    count = y_own.shape[0]
    y = product(inner[...], w_down[...])
    y_own[...] = y[:count]
    for k in range(1, n):
        outs[4 + k][...] = y[k * count : (k + 1) * count].astype(BF)
    core = scalars[1]
    keep, give = split_halves(tn(inner[...], cot[...]), core, columns // 2)
    quarter = columns // 4
    for j in range(2):
        down_keep[j] = keep[j * quarter : (j + 1) * quarter]
        down_give[j] = give[j * quarter : (j + 1) * quarter]
    for b in range(n):
        grads = tn(hidden[:, b * block : (b + 1) * block], acts[...])
        keep, give = split_halves(grads, core, block // 2)
        for j in range(2):
            pair_keep[j, b] = keep[:, j * columns : (j + 1) * columns]
            pair_give[j, b] = give[:, j * columns : (j + 1) * columns]


def norm_back(grad, gain, value):
    scale_row = lax.rsqrt(jnp.mean(value * value, axis=-1, keepdims=True) + EPSILON)
    normed = value * scale_row
    grad_gain = jnp.sum(grad * normed, axis=0, keepdims=True)
    grad = grad * gain
    grad = scale_row * (grad - normed * jnp.mean(grad * normed, axis=-1, keepdims=True))
    return grad, grad_gain


def turn_back_kernel(n, places, *refs):
    scalars, dh_own = refs[:2]
    got = refs[2 : 1 + n]
    middle, gains, cot, w_out, q_ref, k_ref, v_ref, o_ref, lse_ref = refs[1 + n : 10 + n]
    start_ref, cosine_ref, sine_ref = refs[10 + n : 13 + n]
    middle_out, middle_b_out, gain_out, gq_out, keep_out, give_out = refs[13 + n : 19 + n]
    heads, bias = refs[19 + n :]
    count = dh_own.shape[0]
    grad = dh_own[...]
    for piece in got:
        grad = grad + piece[...].astype(F32)
    grad, grad_gain = norm_back(grad, gains[1:2, :], middle[...])
    gain_out[...] = jnp.broadcast_to(grad_gain, gain_out.shape)
    grad = grad + cot[...].astype(F32)
    middle_out[...] = grad
    grad_b = grad.astype(BF)
    middle_b_out[...] = grad_b
    grad_attn = project_back(grad_b, w_out).astype(BF)
    for h in range(HQ):
        part = slice(h % GROUP * count, (h % GROUP + 1) * count)
        heads[h // GROUP, part, :] = grad_attn[:, h * HD : (h + 1) * HD]
    fill_bias(bias, start_ref, scalars, count, places)
    length = 2 * places * count
    cosine, sine = cosine_ref[0:count, :], sine_ref[0:count, :]

    for g in range(HK):
        queries, keys, values, grad = q_ref[g], k_ref[g], v_ref[g], heads[g]
        delta = jnp.sum(grad.astype(F32) * o_ref[g], axis=-1, keepdims=True)
        score = nt(queries, keys) - lse_ref[g]
        score = score.reshape(GROUP, count, length) + bias[...][None]
        prob = jnp.exp(score.reshape(GROUP * count, length))
        grad_values = tn(prob.astype(BF), grad)
        grad_prob = nt(grad, values)
        grad_score = (prob * (grad_prob - delta)).astype(BF)
        dq = product(grad_score, keys) * SCALE
        for j in range(GROUP):
            h = g * GROUP + j
            gq_out[:, h * HD : (h + 1) * HD] = turn(dq[j * count : (j + 1) * count], cosine, -sine)
        grad_keys = tn(grad_score, queries)
        both = jnp.concatenate([grad_keys, grad_values], axis=-1)
        for s in range(places):
            keep_out[s, g] = both[s * count : (s + 1) * count]
            give_out[s, g] = both[(places + s) * count : (places + s + 1) * count].astype(BF)


def padded_rows(block):
    return -(-(block + 1) // 32) * 32


def lanes_of(width):
    return -(-width // 128) * 128


def split_block(grads, gain_row, block, core, keep_ref, give_ref, b):
    rows = padded_rows(block)
    width = lanes_of(grads.shape[1])
    grads = jnp.concatenate([grads, jnp.zeros((block, width - grads.shape[1]), F32)], axis=1)
    tail = jnp.concatenate(
        [gain_row[:, b * block : (b + 1) * block], jnp.zeros((1, width - block), F32)], axis=1
    )
    tail = jnp.concatenate([tail, jnp.zeros((rows - block - 1, width), F32)])
    keep, give = split_halves(jnp.concatenate([grads, tail]), core, rows // 2)
    keep_ref[b] = keep
    give_ref[b] = give


def out_grads_kernel(n, block, scalars, attn, grad_b, gain_row, keep_out, give_out):
    for b in range(n):
        grads = tn(attn[:, b * block : (b + 1) * block], grad_b[...])
        split_block(grads, gain_row[0:1, :], block, scalars[1], keep_out, give_out, b)


def final_kernel(n, block, *refs):
    scalars, kv_own, gq, cosine_ref, sine_ref, weight, hidden, tokens, gains, middle = refs[:10]
    got = refs[10:-4]
    tokens_out, keep_out, give_out, grad_ref = refs[-4:]
    grad_ref[:, : HQ * HD] = gq[...]
    count = gq.shape[0]
    cosine, sine = cosine_ref[0:count, :], sine_ref[0:count, :]
    for h in range(HK):
        total = kv_own[h]
        for piece in got:
            total = total + piece[h].astype(F32)
        base = HQ * HD + h * HD
        grad_ref[:, base : base + HD] = turn(total[:, :HD], cosine, -sine)
        base += HK * HD
        grad_ref[:, base : base + HD] = total[:, HD:].astype(BF)
    grad_qkv = grad_ref[...]
    grad = project_back(grad_qkv, weight)
    grad, grad_gain = norm_back(grad, gains[0:1, :], tokens[...].astype(F32))
    tokens_out[...] = (middle[...] + grad).astype(BF)
    for b in range(n):
        grads = tn(hidden[:, b * block : (b + 1) * block], grad_qkv)
        split_block(grads, grad_gain, block, scalars[1], keep_out, give_out, b)


def fold_kernel(order, keep, recv, own, *gives):
    own[...] = keep[order[0]] + recv[order[0]].astype(F32)
    for j, give in enumerate(gives):
        give[...] = (keep[order[j + 1]] + recv[order[j + 1]].astype(F32)).astype(BF)


def fold(keep, recv, order):
    rest = keep.shape[1:]
    outs = [shape(rest, F32)] + [shape(rest, BF)] * (keep.shape[0] - 1)
    order = jnp.stack([jnp.int32(o) for o in order])
    return call(fold_kernel, [order, keep, recv], outs, [], keep.size)


def pick(stacked, index):
    return lax.dynamic_index_in_dim(stacked, index, 0, keepdims=False)


def joined(mine, other, bit, axis):
    both = jnp.stack([mine, other], axis=axis)
    flipped = jnp.stack([other, mine], axis=axis)
    out = jnp.where(bit == 0, both, flipped)
    shape = mine.shape[:axis] + (2 * mine.shape[axis],) + mine.shape[axis + 1 :]
    return out.reshape(shape)


def layer(
    tokens,
    segment,
    positions,
    norm_attn,
    w_query,
    w_key,
    w_value,
    w_out,
    norm_mlp,
    w_gate,
    w_up,
    w_down,
    cotangent,
):
    count = tokens.shape[1]
    n = lax.axis_size("shard")
    ranks = lax.axis_size("rep")
    places = ranks // 2
    me = lax.axis_index("shard")
    rank = lax.axis_index("rep")
    core = rank % 2
    place = rank // 2
    block = w_query.shape[0]
    half = block // 2
    columns = w_down.shape[0]
    ff = columns * n

    def row_major(value):
        return with_layout_constraint(value, Layout(tuple(range(value.ndim))))

    def send(value, axis, pairs):
        return row_major(lax.ppermute(row_major(value), axis, pairs))

    def across(value, k):
        return send(value, "shard", [(a, a ^ k) for a in range(n)])

    def partner(value):
        return send(value, "rep", [(a, a ^ 1) for a in range(ranks)])

    def place_xor(value, b):
        return send(value, "rep", [(a, a ^ (2 * b)) for a in range(ranks)])

    def place_up(value, s):
        pairs = [(a, a + 2 * s) for a in range(ranks - 2 * s)]
        return send(value, "rep", pairs)

    def place_down(value, s):
        pairs = [(a + 2 * s, a) for a in range(ranks - 2 * s)]
        return send(value, "rep", pairs)

    own_position = positions[0].astype(jnp.int32)
    own_index = rank * count + jnp.arange(count, dtype=jnp.int32)
    starts = own_index - own_position
    held_rank = jnp.stack(key_ranks(places, place, core))
    held_index = (held_rank[1:, None] * count + jnp.arange(count)[None, :]).reshape(-1)
    held_position = jnp.concatenate([own_position, jnp.maximum(held_index - starts[0], 0)])
    cosine_all, sine_all = rope_tables(held_position.astype(F32))
    start = starts[:, None]
    scalars = jnp.stack([me, core, rank, place]).astype(jnp.int32)

    rows = -(-half // 16) * 16

    def half_rows(value):
        return jnp.where(core == 0, value[:rows], value[block - rows :])

    gains_own = jnp.pad(jnp.stack([norm_attn, norm_mlp]), ((0, 14), (0, 0)))
    first = jnp.concatenate([half_rows(w_query), half_rows(w_key), half_rows(w_value)], axis=1)
    first = jnp.concatenate([first, jnp.pad(gains_own, ((0, 0), (0, QKV - block)))])
    got_first = [across(first, k) for k in range(1, n)]
    got_first, cosine_all, sine_all, start, scalars = lax.optimization_barrier(
        (got_first, cosine_all, sine_all, start, scalars)
    )
    rest_first = [partner(g) for g in got_first]

    own_tokens = tokens[0]
    held = [own_tokens] + [place_up(own_tokens, s) for s in range(1, places)]
    held = held + [partner(h) for h in held]
    length = ranks * count

    def columns_of(owner):
        cut = lambda w, b: w[:, b * columns : (b + 1) * columns]
        pairs = [jnp.concatenate([cut(w_gate, b), cut(w_up, b)], axis=1) for b in range(n)]
        return lax.select_n(owner, *pairs)

    own_pair = columns_of(me)
    out_half = half_rows(w_out)
    out_half = jnp.pad(out_half, ((0, 0), (0, lanes_of(D + 2 * columns) - D - 2 * columns)))
    got_second = [
        across(jnp.concatenate([half_rows(columns_of(me ^ k)), out_half], axis=1), k)
        for k in range(1, n)
    ]


    queries, keys, values, attn_heads, lse, attn, hidden1, full_qkv, gains = call(
        functools.partial(front_kernel, n, places, block, rows),
        [scalars, *held, gains_own, w_query, w_key, w_value, *got_first, *rest_first]
        + [cosine_all, sine_all, start],
        [
            shape((HK, GROUP * count, HD), BF),
            shape((HK, length, HD), BF),
            shape((HK, length, HD), BF),
            shape((HK, GROUP * count, HD), F32),
            shape((HK, GROUP * count, 1), F32),
            shape((count, D), BF),
            shape((count, D), BF),
            shape((n, block, QKV), BF),
            shape((8, D), F32),
        ],
        [
            pltpu.VMEM((2 * places, count, D), BF),
            pltpu.VMEM((min(4, 2 * places) * count, D), BF),
            pltpu.VMEM((n, 16, -(-block // 128) * 128), F32),
            pltpu.VMEM((count, length), F32),
        ],
        2 * length * D * 2 * HK * HD,
    )
    attn, got_second, own_cot = lax.optimization_barrier((attn, got_second, cotangent[0]))
    rest_second = [partner(g) for g in got_second]
    got_cot = [across(own_cot, k) for k in range(1, n)]
    middle, hidden2, full_out = call(
        functools.partial(out_kernel, n, block, rows, (2 * columns, 2 * columns + D)),
        [scalars, attn, own_tokens, gains, w_out, *got_second, *rest_second],
        [shape((count, D), F32), shape((count, D), BF), shape((n, block, D), BF)],
        [],
        2 * count * D * D,
    )

    got_hidden2 = [across(hidden2, k) for k in range(1, n)]
    wide = n * count
    mlp_outs = call(
        functools.partial(mlp_kernel, n, block, rows, columns),
        [scalars, hidden2, *got_hidden2, own_cot, *got_cot, own_pair, w_down]
        + [*got_second, *rest_second],
        [
            shape((count, D), F32),
            *[shape((count, D), BF)] * (n - 1),
            shape((wide, columns), BF),
            shape((wide, 2 * columns), BF),
            shape((wide, D), BF),
            shape((wide, D), BF),
        ],
        [pltpu.VMEM((n, block, 2 * columns), BF)],
        2 * wide * D * columns * 5,
    )
    dh_own, dh_send = mlp_outs[0], mlp_outs[1:n]
    inner, acts, wide_hidden2, wide_cot = mlp_outs[n:]
    got_dh = [across(dh_send[k - 1], k) for k in range(1, n)]
    down_keep, down_give, pair_keep, pair_give, y_own, *y_send = call(
        functools.partial(mlp_grads_kernel, n, block, columns),
        [scalars, wide_hidden2, acts, inner, wide_cot, w_down],
        [
            shape((2, columns // 4, D), F32),
            shape((2, columns // 4, D), BF),
            shape((2, n, half, columns), F32),
            shape((2, n, half, columns), BF),
            shape((count, D), F32),
            *[shape((count, D), BF)] * (n - 1),
        ],
        [],
        2 * wide * D * columns * 4,
    )
    odd = place % 2

    def fold_parity(keep, give):
        return fold(keep, partner(give), [odd, 1 - odd])

    down_fold = fold_parity(down_keep, down_give)
    pair_fold = fold_parity(pair_keep, pair_give)
    got_dh, down_fold, pair_fold = lax.optimization_barrier((got_dh, down_fold, pair_fold))
    grad_middle, grad_mid_b, gain_mlp_row, gq, kv_keep, kv_give = call(
        functools.partial(turn_back_kernel, n, places),
        [scalars, dh_own, *got_dh, middle, gains, own_cot, full_out, queries, keys, values]
        + [attn_heads, lse, start, cosine_all, sine_all],
        [
            shape((count, D), F32),
            shape((count, D), BF),
            shape((8, D), F32),
            shape((count, D), BF),
            shape((places, HK, count, 2 * HD), F32),
            shape((places, HK, count, 2 * HD), BF),
        ],
        [pltpu.VMEM((HK, GROUP * count, HD), BF), pltpu.VMEM((count, length), F32)],
        10 * HQ * count * length * HD,
    )
    kv_sums = fold(kv_keep, partner(kv_give), list(range(places)))
    got_kv = [place_down(kv_sums[s], s) for s in range(1, places)]
    y_total = y_own
    for k in range(1, n):
        y_total = y_total + across(y_send[k - 1], k).astype(F32)
    result = (middle + y_total).astype(BF)
    padded = padded_rows(block)
    out_keep, out_give = call(
        functools.partial(out_grads_kernel, n, block),
        [scalars, attn, grad_mid_b, gain_mlp_row],
        [shape((n, padded // 2, lanes_of(D)), kind) for kind in (F32, BF)],
        [],
        2 * count * D * D,
    )

    def fold_blocks(keep, give):
        return fold(keep, partner(give), [me ^ k for k in range(n)])

    out_fold = fold_blocks(out_keep, out_give)
    out_fold, gq = lax.optimization_barrier((out_fold, gq))
    grad_inputs, qkv_keep, qkv_give = call(
        functools.partial(final_kernel, n, block),
        [scalars, kv_sums[0], gq, cosine_all, sine_all, full_qkv, hidden1, own_tokens, gains, grad_middle]
        + got_kv,
        [
            shape((count, D), BF),
            *[shape((n, padded // 2, lanes_of(QKV)), kind) for kind in (F32, BF)],
        ],
        [pltpu.VMEM((count, QKV), BF)],
        4 * count * D * QKV,
    )

    def over_places(keep, give):
        total = keep + place_xor(give, 1).astype(F32)
        b = 2
        while b < places:
            mine = total.astype(BF)
            total = mine.astype(F32) + place_xor(mine, b).astype(F32)
            b *= 2
        return total.astype(BF)

    def finish(mine):
        mine = joined(mine, place_xor(mine, 1), odd, 0)
        return joined(mine, partner(mine), core, 0)

    grad_down = finish(over_places(*down_fold)).astype(F32)

    grad_pair = over_places(*pair_fold)
    pair_rows = jnp.zeros((half, ff), BF)
    for k in range(n):
        part = pick(grad_pair, me ^ k)
        part = across(part, k) if k else part
        pair_rows = lax.dynamic_update_slice_in_dim(pair_rows, part, (me ^ k) * columns, 1)
    other = place_xor(pair_rows, 1)
    pair_rows = jnp.where(
        odd == 0, jnp.stack([pair_rows, other]), jnp.stack([other, pair_rows])
    )
    pair_rows = joined(pair_rows, partner(pair_rows), core, 1).astype(F32)
    grad_gate, grad_up = pair_rows[0], pair_rows[1]

    def reduce_all(total, *gives):
        for k, give in enumerate(gives, 1):
            total = total + across(give, k).astype(F32)
        total = total.reshape(2, padded // 4, total.shape[1])
        keep, give = pick(total, odd), pick(total, 1 - odd).astype(BF)
        return finish(over_places(keep, give)).astype(F32)

    out_sum = reduce_all(*out_fold)
    qkv_sum = reduce_all(*fold_blocks(qkv_keep, qkv_give))

    q_end, k_end = HQ * HD, (HQ + HK) * HD
    return (
        result[None],
        grad_inputs[None],
        qkv_sum[block, :block],
        qkv_sum[:block, :q_end],
        qkv_sum[:block, q_end:k_end],
        qkv_sum[:block, k_end:QKV],
        out_sum[:block, :D],
        out_sum[block, :block],
        grad_gate,
        grad_up,
        grad_down,
    )


def solution(mesh):
    rows = P("shard", None)
    placed = (
        P("shard", "rep", None),
        P("shard", "rep"),
        P("shard", "rep"),
        P("shard"),
        rows,
        rows,
        rows,
        rows,
        P("shard"),
        rows,
        rows,
        rows,
        P("shard", "rep", None),
    )
    outputs = (
        P("shard", "rep", None),
        P("shard", "rep", None),
        P("shard"),
        rows,
        rows,
        rows,
        rows,
        P("shard"),
        rows,
        rows,
        rows,
    )
    return jax.shard_map(layer, mesh=mesh, in_specs=placed, out_specs=outputs, check_vma=False)
```
